32 devices in a mesh: section: 2 (over core), fsdp: 4 (over z), dp: 4 (over y, x).
Axes of the slice: x: 2, y: 2, z: 4, core: 2. Of those that a mesh axis runs over, the one named last changes fastest.
Arguments:
- tokens: bfloat16 [1, 16, 128, 1024], P(None, ('fsdp', 'dp')), may hold values from -6 to 6
- segments: int32 [1, 16, 128], P(None, ('fsdp', 'dp')), may hold values from 0 to 3, never falling along the last dimension, each value on 1 to 64 neighbouring positions
- cotangent: float32 [1, 16, 128, 1024], P(None, ('fsdp', 'dp')), may hold values from -6 to 6
- norm_gains: bfloat16 [2, 2, 1024], P('section', None, 'fsdp'), may hold values from 0.5 to 1.5
- proj_weight: bfloat16 [2, 1024, 3072], P('section', 'fsdp'), may hold values from -0.1875 to 0.1875
- rate_weight: bfloat16 [2, 1024, 8], P('section', 'fsdp'), may hold values from -0.1875 to 0.1875
- out_weight: bfloat16 [2, 1024, 1024], P('section', 'fsdp'), may hold values from -0.375 to 0.375
- up_weight: bfloat16 [2, 1024, 5632], P('section', 'fsdp'), may hold values from -0.1875 to 0.1875
- down_weight: bfloat16 [2, 1024, 2816], P('section', 'fsdp'), may hold values from -0.21875 to 0.21875
- conv_kernels: float32 [2, 4, 2048], P('section'), may hold values from -3 to 3
- head_params: float32 [2, 2, 4], P('section'), may hold values from -2.5 to 0.5
- out_gain: float32 [2, 256], P('section'), may hold values from 0.5 to 1.5
Outputs:
- section_output: bfloat16 [2, 1, 16, 128, 1024], P('section', None, ('fsdp', 'dp'))
- input_grad: float32 [2, 1, 16, 128, 1024], P('section', None, ('fsdp', 'dp'))
- gains_grad: float32 [2, 2, 1024], P('section', None, 'fsdp')
- proj_grad: float32 [2, 1024, 3072], P('section', 'fsdp')
- rate_grad: float32 [2, 1024, 8], P('section', 'fsdp')
- out_grad: float32 [2, 1024, 1024], P('section', 'fsdp')
- up_grad: float32 [2, 1024, 5632], P('section', 'fsdp')
- down_grad: float32 [2, 1024, 2816], P('section', 'fsdp')
- kernel_grad: float32 [2, 4, 2048], P('section')
- head_grad: float32 [2, 2, 4], P('section')
- out_gain_grad: float32 [2, 256], P('section')
The draws below stay inside these ranges and needn't reach their ends.
Inputs may be any that keep to these rules, and one draw needn't show every extreme that they name: `segments`: within each sequence the numbers never fall, every one of 0 .. 3 occurs, and each document holds 1 to 64 positions, one exactly 64.
All inputs are finite; a program needn't handle non-finite values.
Results may differ from the reference program's by a relative error of at most 0.034.
Values may be sent and summed in bfloat16 or wider, within the bound.
A program may use at most 256 MiB of HBM per device.

```python
import math
from functools import partial
import jax
import jax.numpy as jnp
import numpy as np
from jax import lax

D = 1024
H = 4
DK = 128
DV = 256
FF = 2816
CONV = 4
SPAN = 64
DOCS = 4
MB = 1
SEQ = 128
SEQS = 16


def block_levels(key, extent, shards, least, high):
    level, own = 1.0, jax.random.fold_in(key, 6)
    for dim, shards_of in shards:
        steps = jnp.exp(jax.random.uniform(jax.random.fold_in(own, dim), (shards_of,), jnp.float32, least / len(shards), high / len(shards)))
        level = level * jnp.repeat(steps, extent[dim] // shards_of).reshape([-1 if axis == dim else 1 for axis in range(len(extent))])
    return level


def split_up(count, total, reach, skew):
    loads = [(1 << 20) // math.isqrt(rank ** skew) + 1 for rank in range(2, count + 1)]
    spare, holding = total - reach - (count - 1), [1] * (count - 1)
    while spare > 0:
        candidates = [i for i in range(count - 1) if holding[i] < reach]
        mass, budget = sum([loads[i] for i in candidates]), spare
        for i in candidates:
            more = min(reach - holding[i], max(1, budget * loads[i] // mass), spare)
            holding[i] = holding[i] + more
            spare = spare - more
    return np.array([reach] + holding)


def uneven_parts(rng, amount, total, most, skew):
    if amount == 2:
        one = jax.random.randint(rng, (), max(1, total - most), min(most, total - 1) + 1)
        return jnp.stack([one, total - one])
    lengths = jnp.asarray(split_up(amount, total, most, skew), jnp.int32)
    couples = (amount - 1) // 2
    source_of, taker = lengths[1:1 + 2 * couples:2], lengths[2:2 + 2 * couples:2]
    slack = jnp.minimum(source_of - 1, most - taker)
    moved = jax.random.randint(jax.random.fold_in(rng, 1), (couples,), 0, 1 << 20) % (slack + 1)
    lengths = lengths.at[1:1 + 2 * couples:2].set(source_of - moved).at[2:2 + 2 * couples:2].set(taker + moved)
    return lengths[jax.random.permutation(jax.random.fold_in(rng, 2), amount)]


def centred(rng, shape, deviation, reach, split=(), kind=jnp.bfloat16):
    loudness = block_levels(rng, shape, split, -0.22, 0.18) if split else 1.0
    drawn = jax.random.normal(rng, shape, jnp.float32) * deviation * loudness
    return jnp.minimum(jnp.maximum(drawn, -reach), reach).astype(kind)


def setup_inputs(seed: int = 0) -> dict:
    streams_of = jax.random.split(jax.random.key(seed), 13)
    return {
        "tokens": centred(streams_of[0], (MB, SEQS, SEQ, D), 1.0, 6.0, ((1, 16),)),
        "segments": jax.vmap(lambda own: jnp.searchsorted(jnp.cumsum(uneven_parts(own, DOCS, SEQ, SEQ // 2, 1)), jnp.arange(SEQ), side="right"))(jax.random.split(streams_of[1], MB * SEQS)).reshape((MB, SEQS, SEQ)).astype(jnp.int32),
        "cotangent": centred(streams_of[2], (MB, SEQS, SEQ, D), 1.0, 6.0, ((1, 16),), jnp.float32),
        "norm_gains": jnp.clip(1.0 + 0.1 * jax.random.normal(streams_of[3], (2, 2, D), jnp.float32), 0.5, 1.5).astype(jnp.bfloat16),
        "proj_weight": centred(streams_of[4], (2, D, 2 * H * DK + 2 * H * DV), D ** -0.5, 0.1875, ((0, 2), (1, 4))),
        "rate_weight": centred(streams_of[5], (2, D, 2 * H), D ** -0.5, 0.1875, ((0, 2), (1, 4))),
        "out_weight": centred(streams_of[6], (2, D, H * DV), (H * DV // 4) ** -0.5, 0.375, ((0, 2), (1, 4))),
        "up_weight": centred(streams_of[7], (2, D, 2 * FF), D ** -0.5, 0.1875, ((0, 2), (1, 4))),
        "down_weight": centred(streams_of[8], (2, D, FF), (FF // 4) ** -0.5, 0.21875, ((0, 2), (1, 4))),
        "conv_kernels": centred(streams_of[9], (2, CONV, 2 * H * DK + H * DV), 0.5, 3.0, ((0, 2),), jnp.float32),
        "head_params": jnp.clip(-2.5 + 3.0 * jax.random.uniform(streams_of[10], (2, 2, H), jnp.float32) ** block_levels(streams_of[10], (2, 2, H), ((0, 2),), -0.2, 0.2), -2.5, 0.5),
        "out_gain": jnp.clip(1.0 + 0.1 * jax.random.normal(streams_of[11], (2, DV), jnp.float32), 0.5, 1.5),
    }


highest = lax.Precision.HIGHEST
reset_level = -30.0

def rms_gain(values, gain_vec):
    return values * lax.rsqrt(lax.optimization_barrier(jnp.mean(values * values, -1, keepdims=True)) + 1e-06) * gain_vec

def swiglu(joined):
    half_width = joined.shape[-1] // 2
    return jax.nn.silu(joined[..., :half_width]) * joined[..., half_width:]

def short_conv(raw_input, kernel, segment):
    length = raw_input.shape[1]
    tap_count = kernel.shape[0]
    total = raw_input * kernel[tap_count - 1]
    for offset in range(1, tap_count):
        shifted = jnp.pad(raw_input, ((0, 0), (offset, 0), (0, 0)))[:, :length]
        earlier = jnp.pad(segment, ((0, 0), (offset, 0)), constant_values=-1)[:, :length]
        total = total + jnp.where((earlier == segment)[..., None], shifted, 0.0) * kernel[tap_count - 1 - offset]
    return jax.nn.silu(total)

def delta_rule(queries, key_rows, value_rows, beta_gate, decays, block_len):
    batch_size, head_count, length, key_dim = queries.shape
    value_dim = value_rows.shape[-1]
    block_count = length // block_len

    def to_blocks(array):
        return array.reshape(array.shape[:2] + (block_count, block_len) + array.shape[3:])
    queries = to_blocks(queries)
    key_rows = to_blocks(key_rows)
    value_rows = to_blocks(value_rows)
    beta_gate = to_blocks(beta_gate)
    levels = jnp.cumsum(to_blocks(decays), axis=-1)
    places = jnp.arange(block_len)
    lower_mask = places[:, None] >= places[None, :]
    strict_mask = places[:, None] > places[None, :]
    spread = jnp.exp(jnp.where(lower_mask, levels[..., :, None] - levels[..., None, :], -1e+30))
    beta_keys = key_rows * beta_gate[..., None]
    key_inner = jnp.einsum('bhncd,bhnmd->bhncm', beta_keys, key_rows, precision=highest) * spread
    system = jnp.where(strict_mask, key_inner, 0.0)
    right_side = jnp.concatenate([beta_keys * jnp.exp(levels)[..., None], value_rows * beta_gate[..., None]], -1)
    solved = lax.linalg.triangular_solve(system, right_side, left_side=True, lower=True, unit_diagonal=True)
    solved_keys = solved[..., :key_dim]
    solved_values = solved[..., key_dim:]
    scores = jnp.einsum('bhncd,bhnmd->bhncm', queries, key_rows, precision=highest) * spread
    fading = queries * jnp.exp(levels)[..., None]
    final_level = levels[..., -1:]
    carried = key_rows * jnp.exp(final_level - levels)[..., None]

    def advance(memory, pieces):
        fading_part, keys_part, values_part, scores_part, carried_part, final_part = pieces
        update = values_part - jnp.einsum('bhcd,bhde->bhce', keys_part, memory, precision=highest)
        output = jnp.einsum('bhcd,bhde->bhce', fading_part, memory, precision=highest) + jnp.einsum('bhcm,bhme->bhce', scores_part, update, precision=highest)
        memory = memory * jnp.exp(final_part)[..., None] + jnp.einsum('bhcd,bhce->bhde', carried_part, update, precision=highest)
        return (memory, output)
    pieces = tuple((jnp.moveaxis(array, 2, 0) for array in (fading, solved_keys, solved_values, scores, carried, final_level)))
    initial = jnp.zeros((batch_size, head_count, key_dim, value_dim), queries.dtype)
    _, outputs = lax.scan(advance, initial, pieces)
    return jnp.moveaxis(outputs, 0, 2).reshape(batch_size, head_count, length, value_dim)

def token_mixer(projected, rate_logits, kernel, head_params, out_gain, segment):
    batch_size, length, _ = projected.shape
    head_count = head_params.shape[1]
    value_dim = out_gain.shape[0]
    channels = kernel.shape[1]
    key_width = (channels - head_count * value_dim) // 2
    key_dim = key_width // head_count
    mixed = short_conv(projected[..., :channels], kernel, segment)

    def heads_of(array, size):
        return jnp.moveaxis(array.reshape(batch_size, length, head_count, size), 2, 1)
    queries = heads_of(mixed[..., :key_width], key_dim)
    key_rows = heads_of(mixed[..., key_width:2 * key_width], key_dim)
    value_rows = heads_of(mixed[..., 2 * key_width:], value_dim)
    queries = queries * lax.rsqrt(lax.optimization_barrier(jnp.sum(queries * queries, -1, keepdims=True)) + 1e-06) * key_dim ** (-0.5)
    key_rows = key_rows * lax.rsqrt(lax.optimization_barrier(jnp.sum(key_rows * key_rows, -1, keepdims=True)) + 1e-06)
    beta_gate = jax.nn.sigmoid(jnp.moveaxis(rate_logits[..., head_count:], 2, 1))
    decays = -jnp.exp(head_params[0])[:, None] * jax.nn.softplus(jnp.moveaxis(rate_logits[..., :head_count], 2, 1) + head_params[1][:, None])
    earlier = jnp.pad(segment, ((0, 0), (1, 0)), constant_values=-1)[:, :length]
    decays = jnp.where((earlier != segment)[:, None, :], reset_level, decays)
    output = delta_rule(queries, key_rows, value_rows, beta_gate, decays, SPAN)
    output = output * lax.rsqrt(lax.optimization_barrier(jnp.mean(output * output, -1, keepdims=True)) + 1e-05) * out_gain
    gating = heads_of(projected[..., channels:], value_dim)
    return jnp.moveaxis(output * jax.nn.silu(gating), 1, 2).reshape(batch_size, length, head_count * value_dim)

def last_contract(left, right):
    return lax.dot_general(left.astype(jnp.float32), right.astype(jnp.float32), (((2,), (1,)), ((), ())), preferred_element_type=jnp.float32)

def layer_forward(entering, segment, weights, small_params):
    norm_gains, proj_weight, rate_weight, out_weight, up_weight, down_weight = weights
    kernel, head_params, out_gain = small_params
    widened = entering.astype(jnp.float32)
    normed_one, norm_one_back = jax.vjp(rms_gain, widened, norm_gains[0].astype(jnp.float32))
    hidden_one = normed_one.astype(jnp.bfloat16)
    projected = jnp.dot(hidden_one.astype(jnp.float32), proj_weight.astype(jnp.float32), preferred_element_type=jnp.float32)
    rate_logits = jnp.dot(hidden_one.astype(jnp.float32), rate_weight.astype(jnp.float32), preferred_element_type=jnp.float32)
    mixed_out, mixer_back = jax.vjp(partial(token_mixer, segment=segment), projected, rate_logits, kernel, head_params, out_gain)
    mixed_half = mixed_out.astype(jnp.bfloat16)
    stream = widened + last_contract(mixed_half, out_weight)
    normed_two, norm_two_back = jax.vjp(rms_gain, stream, norm_gains[1].astype(jnp.float32))
    hidden_two = normed_two.astype(jnp.bfloat16)
    gate_up = jnp.dot(hidden_two.astype(jnp.float32), up_weight.astype(jnp.float32), preferred_element_type=jnp.float32)
    activated, act_back = jax.vjp(swiglu, gate_up)
    act_half = activated.astype(jnp.bfloat16)
    layer_out = (stream + last_contract(act_half, down_weight)).astype(jnp.bfloat16)
    residuals = (norm_one_back, hidden_one, mixer_back, mixed_half, norm_two_back, hidden_two, act_back, act_half)
    return (layer_out, residuals)

def layer_backward(cotangent_in, residuals, weights):
    norm_gains, proj_weight, rate_weight, out_weight, up_weight, down_weight = weights
    norm_one_back, hidden_one, mixer_back, mixed_half, norm_two_back, hidden_two, act_back, act_half = residuals
    dout_half = cotangent_in.astype(jnp.bfloat16)
    gate_up_grad, = act_back(jnp.dot(dout_half.astype(jnp.float32), down_weight.astype(jnp.float32), preferred_element_type=jnp.float32))
    gate_up_cot = gate_up_grad.astype(jnp.bfloat16)
    stream_grad, gain_two = norm_two_back(last_contract(gate_up_cot, up_weight))
    stream_grad = cotangent_in + stream_grad
    branch_cot = stream_grad.astype(jnp.bfloat16)
    proj_grad, rate_grad, kernel_grad, head_grad, out_gain_grad = mixer_back(jnp.dot(branch_cot.astype(jnp.float32), out_weight.astype(jnp.float32), preferred_element_type=jnp.float32))
    proj_cot = proj_grad.astype(jnp.bfloat16)
    rate_cot = rate_grad.astype(jnp.bfloat16)
    hidden_grad = last_contract(proj_cot, proj_weight) + last_contract(rate_cot, rate_weight)
    entry_grad, gain_one = norm_one_back(hidden_grad)
    pairs = (hidden_one, proj_cot, rate_cot, mixed_half, branch_cot, hidden_two, gate_up_cot, act_half, dout_half)
    return (stream_grad + entry_grad, pairs, (kernel_grad, head_grad, out_gain_grad), jnp.stack([gain_one, gain_two]))

def weight_terms(pairs, gain_sum, start, count):
    flattened = [member.reshape(-1, member.shape[-1]) for member in pairs]
    hidden_one, proj_cot, rate_cot, mixed_half, branch_cot, hidden_two, gate_up_cot, act_half, dout_half = flattened

    def rows_of(matrix):
        return lax.dynamic_slice_in_dim(matrix, start, count, 1)

    def product(left, right):
        return lax.dot_general(left.astype(jnp.float32), right.astype(jnp.float32), (((0,), (0,)), ((), ())), preferred_element_type=jnp.float32)
    own_hidden = rows_of(hidden_one)
    return jnp.concatenate([product(own_hidden, proj_cot), product(own_hidden, rate_cot), product(rows_of(branch_cot), mixed_half), product(rows_of(hidden_two), gate_up_cot), product(rows_of(dout_half), act_half), rows_of(gain_sum).T], 1)

def split_term(total, widths):
    pieces = []
    column = 0
    for width in widths:
        pieces.append(total[..., column:column + width])
        column = column + width
    return pieces

def reference(tokens, segments, cotangent, norm_gains, proj_weight, rate_weight, out_weight, up_weight, down_weight, conv_kernels, head_params, out_gain):

    def weights_of(index):
        return (norm_gains[index], proj_weight[index], rate_weight[index], out_weight[index], up_weight[index], down_weight[index])

    def small_of(index):
        return (conv_kernels[index], head_params[index], out_gain[index])
    row_count = proj_weight.shape[1]
    widths = [proj_weight.shape[2], rate_weight.shape[2], out_weight.shape[2], up_weight.shape[2], down_weight.shape[2], 2]
    term_width = sum(widths)

    def one_batch(carry, inputs):
        entering, segment, incoming = inputs
        middle, saved_zero = layer_forward(entering, segment, weights_of(0), small_of(0))
        leaving, saved_one = layer_forward(middle, segment, weights_of(1), small_of(1))
        grad_middle, pairs_one, small_one, gains_one = layer_backward(incoming, saved_one, weights_of(1))
        grad_entry, pairs_zero, small_zero, gains_zero = layer_backward(grad_middle, saved_zero, weights_of(0))
        terms = jnp.stack([weight_terms(pairs_zero, gains_zero, 0, row_count), weight_terms(pairs_one, gains_one, 0, row_count)])
        smalls = tuple((carry[1][i] + jnp.stack([small_zero[i], small_one[i]]) for i in range(3)))
        return ((carry[0] + terms, smalls), (jnp.stack([middle, leaving]), jnp.stack([grad_entry, grad_middle])))
    initial = (jnp.zeros((2, row_count, term_width), jnp.float32), (jnp.zeros(conv_kernels.shape, jnp.float32), jnp.zeros(head_params.shape, jnp.float32), jnp.zeros(out_gain.shape, jnp.float32)))
    final, stacked = lax.scan(one_batch, initial, (tokens, segments, cotangent))
    totals, smalls = final
    section_output = jnp.moveaxis(stacked[0], 1, 0)
    input_grad = jnp.moveaxis(stacked[1], 1, 0)
    pieces = split_term(totals, widths)
    gains_grad = jnp.transpose(pieces[5], (0, 2, 1))
    return (section_output, input_grad, gains_grad, pieces[0], pieces[1], pieces[2], pieces[3], pieces[4], smalls[0], smalls[1], smalls[2])
```

```python
from functools import partial

import jax
import jax.numpy as jnp
from jax import lax
from jax.experimental import pallas as pl
from jax.experimental.pallas import tpu as pltpu
from jax.sharding import PartitionSpec as P

SPAN = 64
LANES = 128

reset_level = -30.0
bf16 = jnp.bfloat16
f32 = jnp.float32


def dots(left, right, dims):
    return lax.dot_general(
        left, right, (dims, ((), ())), precision=lax.Precision.HIGHEST, preferred_element_type=f32
    )


def mm(left, right):
    return dots(left, right, ((1,), (0,)))


def mt(left, right):
    return dots(left, right, ((1,), (1,)))


def tm(left, right):
    return dots(left, right, ((0,), (0,)))


def rowsum(value):
    return jnp.sum(value, -1, keepdims=True)


def colsum(value):
    return jnp.sum(value, 0, keepdims=True)


def sequence_of(ref, q, odd, parts):
    return jnp.concatenate([ref[parts * q + (p ^ odd)] for p in range(parts)], 0)


def masks_of(length):
    rows = lax.broadcasted_iota(jnp.int32, (length, length), 0)
    columns = lax.broadcasted_iota(jnp.int32, (length, length), 1)
    same = (rows // SPAN) == (columns // SPAN)
    return rows, columns, same & (rows >= columns), same & (rows > columns), rows == columns, same


def conv_of(raw, seg, taps):
    length, count = raw.shape[0], taps.shape[0]
    places = lax.broadcasted_iota(jnp.int32, (length, 1), 0)
    total = raw * taps[count - 1 : count]
    kept = []
    for offset in range(1, count):
        shifted = pltpu.roll(raw, offset, 0)
        keep = (places >= offset) & (pltpu.roll(seg, offset, 0) == seg)
        kept.append((keep, shifted))
        total = total + jnp.where(keep, shifted, 0.0) * taps[count - 1 - offset : count - offset]
    return total, kept


def softplus(value):
    return jnp.maximum(value, 0.0) + jnp.log1p(jnp.exp(-jnp.abs(value)))


def prepared(joined, seg, taps, scale_log, bias, sizes, masks):
    key_dim, value_dim = sizes
    channels = 2 * key_dim + value_dim
    rows, columns, lower, strict, eye, same = masks
    length = joined.shape[0]
    raw = joined[:, :channels]
    gate = joined[:, channels : channels + value_dim]
    tail = joined[:, channels + value_dim :]
    total, kept = conv_of(raw, seg, taps)
    sig = jax.nn.sigmoid(total)
    mixed = total * sig
    qm, km, v = mixed[:, :key_dim], mixed[:, key_dim : 2 * key_dim], mixed[:, 2 * key_dim :]
    rq = lax.rsqrt(rowsum(qm * qm) + 1e-06)
    rk = lax.rsqrt(rowsum(km * km) + 1e-06)
    q = qm * rq * key_dim ** (-0.5)
    k = km * rk
    beta = jax.nn.sigmoid(tail[:, 1:2])
    pre = tail[:, 0:1] + bias
    places = lax.broadcasted_iota(jnp.int32, (length, 1), 0)
    start = (places == 0) | (pltpu.roll(seg, 1, 0) != seg)
    free_decay = -jnp.exp(scale_log) * softplus(pre)
    decay = jnp.where(start, reset_level, free_decay)
    decay_row = colsum(jnp.where(eye, decay, 0.0))
    lev = rowsum(jnp.where(lower, decay_row, 0.0))
    fin = rowsum(jnp.where(same, decay_row, 0.0))
    lev_row = colsum(jnp.where(eye, lev, 0.0))
    spread = jnp.exp(jnp.where(lower, lev - lev_row, -1e30))
    grow = jnp.exp(lev)
    left = jnp.exp(fin - lev)
    return dict(
        raw=raw, gate=gate, total=total, kept=kept, sig=sig, rq=rq, rk=rk, q=q, k=k, v=v, beta=beta,
        pre=pre, start=start, free_decay=free_decay, spread=spread, grow=grow, left=left, fin=fin,
        bk=k * beta,
    )


def advance(p, solved, scores, key_dim, length):
    memory, memories, updates, outs = None, [], [], []
    for block in range(length // SPAN):
        part = slice(block * SPAN, (block + 1) * SPAN)
        update = solved[part, key_dim:]
        if memory is not None:
            update = update - mm(solved[part, :key_dim], memory)
        out = mm(scores[part, part], update)
        if memory is not None:
            out = out + mm((p["q"] * p["grow"])[part], memory)
        memories.append(memory)
        updates.append(update)
        outs.append(out)
        if (block + 1) * SPAN < length:
            grown = tm((p["k"] * p["left"])[part], update)
            if memory is not None:
                grown = grown + memory * jnp.exp(p["fin"][block * SPAN : block * SPAN + 1])
            memory = grown
    return memories, updates, jnp.concatenate(outs, 0)


def mixer_forward_kernel(sizes, odd_ref, joined_ref, seg_ref, taps_ref, head_ref, gain_ref,
                         out_ref, inverse_ref, solved_ref):
    key_dim, value_dim = sizes
    pieces, rows_each, _ = joined_ref.shape
    parts = 2
    length = parts * rows_each
    odd = odd_ref[0]
    masks = masks_of(length)
    rows, columns, lower, strict, eye, same = masks
    taps = taps_ref[...]
    scale_log, bias = head_ref[0:1, :], head_ref[1:2, :]
    for s in range(pieces // parts):
        joined = sequence_of(joined_ref, s, odd, parts)
        seg = sequence_of(seg_ref, s, odd, parts)
        p = prepared(joined, seg, taps, scale_log, bias, sizes, masks)
        system = jnp.where(strict, mt(p["bk"], p["k"]) * p["spread"], 0.0)
        inverse = None
        half = 1
        while half < SPAN:
            joins = ((rows // half) % 2 == 1) & (columns // half == rows // half - 1)
            corner = jnp.where(joins, system, 0.0)
            if inverse is None:
                inverse = jnp.where(eye, 1.0, 0.0) - corner
            else:
                inverse = inverse - mm(inverse, mm(corner, inverse))
            half = half * 2
        solved = mm(inverse, jnp.concatenate([p["bk"] * p["grow"], p["v"] * p["beta"]], 1))
        scores = mt(p["q"], p["k"]) * p["spread"]
        _, _, o = advance(p, solved, scores, key_dim, length)
        o = o * lax.rsqrt(jnp.mean(o * o, -1, keepdims=True) + 1e-05) * gain_ref[...]
        y = (o * (p["gate"] * jax.nn.sigmoid(p["gate"]))).astype(out_ref.dtype)
        inverse_ref[s] = inverse
        solved_ref[s] = solved
        for part in range(parts):
            out_ref[parts * s + (part ^ odd)] = y[part * rows_each : (part + 1) * rows_each]


def mixer_backward_kernel(sizes, odd_ref, joined_ref, seg_ref, taps_ref, head_ref, gain_ref,
                          inverse_ref, solved_ref, dy_ref, cot_ref, taps_grad_ref, small_ref):
    key_dim, value_dim = sizes
    pieces, rows_each, width = joined_ref.shape
    parts = 2
    length = parts * rows_each
    odd = odd_ref[0]
    masks = masks_of(length)
    rows, columns, lower, strict, eye, same = masks
    taps = taps_ref[...]
    count = taps.shape[0]
    scale_log, bias = head_ref[0:1, :], head_ref[1:2, :]
    taps_grad = jnp.zeros(taps.shape, f32)
    gain_grad = jnp.zeros((1, value_dim), f32)
    scale_grad = jnp.zeros((1, 1), f32)
    bias_grad = jnp.zeros((1, 1), f32)
    lane = lax.broadcasted_iota(jnp.int32, (length, width - 2 * key_dim - 2 * value_dim), 1)
    for s in range(pieces // parts):
        joined = sequence_of(joined_ref, s, odd, parts)
        seg = sequence_of(seg_ref, s, odd, parts)
        dy = sequence_of(dy_ref, s, odd, parts)
        p = prepared(joined, seg, taps, scale_log, bias, sizes, masks)
        q, k, v, bk, beta, grow, left = (p[n] for n in ("q", "k", "v", "bk", "beta", "grow", "left"))
        inverse, solved = inverse_ref[s], solved_ref[s]
        gram = mt(bk, k) * p["spread"]
        scores = mt(q, k) * p["spread"]
        memories, updates, o = advance(p, solved, scores, key_dim, length)
        r = lax.rsqrt(jnp.mean(o * o, -1, keepdims=True) + 1e-05)
        on = o * r
        gate_sig = jax.nn.sigmoid(p["gate"])
        gate_act = p["gate"] * gate_sig
        gained = dy * gain_ref[...]
        gain_grad = gain_grad + colsum(dy * on * gate_act)
        dgate = gained * on * (gate_sig * (1.0 + p["gate"] * (1.0 - gate_sig)))
        don = gained * gate_act
        do = r * (don - on * jnp.mean(don * on, -1, keepdims=True))
        fading, carried = q * grow, k * left
        dmemory = None
        zeros_k = jnp.zeros((SPAN, key_dim), f32)
        dfading, dsolved, dscores, dcarried, dfin = [], [], [], [], []
        blocks = length // SPAN
        for block in reversed(range(blocks)):
            part = slice(block * SPAN, (block + 1) * SPAN)
            memory, update, dout = memories[block], updates[block], do[part]
            dupdate = tm(scores[part, part], dout)
            dfin_own = jnp.zeros((1, 1), f32)
            dcarried_own = zeros_k
            later = dmemory
            if later is not None:
                dupdate = dupdate + mm(carried[part], later)
                dcarried_own = mt(update, later)
            dscores_own = mt(dout, update)
            fill = [jnp.zeros((SPAN, SPAN), f32)] * blocks
            fill[block] = dscores_own
            if memory is not None:
                dfading_own = mt(dout, memory)
                dkeys_own = -mt(dupdate, memory)
                dmemory = tm(fading[part], dout) - tm(solved[part, :key_dim], dupdate)
                if later is not None:
                    fade = jnp.exp(p["fin"][block * SPAN : block * SPAN + 1])
                    dmemory = dmemory + later * fade
                    dfin_own = colsum(rowsum(later * memory)) * fade
            else:
                dfading_own, dkeys_own = zeros_k, zeros_k
            dfading.insert(0, dfading_own)
            dsolved.insert(0, jnp.concatenate([dkeys_own, dupdate], 1))
            dscores.insert(0, jnp.concatenate(fill, 1))
            dcarried.insert(0, dcarried_own)
            dfin.insert(0, jnp.broadcast_to(dfin_own, (SPAN, 1)))
        dfading, dsolved, dscores, dcarried, dfin = (
            jnp.concatenate(own, 0) for own in (dfading, dsolved, dscores, dcarried, dfin)
        )
        right = tm(inverse, dsolved)
        dsystem = -jnp.where(strict, mt(right, solved), 0.0)
        right_k, right_v = right[:, :key_dim], right[:, key_dim:]
        dlev = rowsum(right_k * bk) * grow
        dbk = right_k * grow
        dv = right_v * beta
        dbeta = rowsum(right_v * v)
        dgram = dsystem * p["spread"]
        dbk = dbk + mm(dgram, k)
        dk = tm(dgram, bk)
        dinner = dscores * p["spread"]
        dq = mm(dinner, k) + dfading * grow
        dk = dk + tm(dinner, q)
        dlevel = dsystem * gram + dscores * scores
        dlev = dlev + rowsum(dlevel) - rowsum(jnp.where(eye, colsum(dlevel), 0.0))
        dlev = dlev + rowsum(dfading * fading)
        spent = rowsum(dcarried * carried)
        dk = dk + dcarried * left
        dlev = dlev - spent
        dk = dk + dbk * beta
        dbeta = dbeta + rowsum(dbk * k)
        spent_row = colsum(jnp.where(eye, spent, 0.0))
        dlev_row = colsum(jnp.where(eye, dlev, 0.0))
        upper = same & (rows <= columns)
        ddecay = rowsum(jnp.where(upper, dlev_row, 0.0)) + rowsum(jnp.where(same, spent_row, 0.0)) + dfin
        ddecay = jnp.where(p["start"], 0.0, ddecay)
        drate = ddecay * -jnp.exp(scale_log) * jax.nn.sigmoid(p["pre"])
        scale_grad = scale_grad + colsum(ddecay * p["free_decay"])
        bias_grad = bias_grad + colsum(drate)
        dwrite = dbeta * beta * (1.0 - beta)
        qn = q * key_dim**0.5
        dqm = p["rq"] * key_dim ** (-0.5) * (dq - qn * rowsum(dq * qn))
        dkm = p["rk"] * (dk - k * rowsum(dk * k))
        dmixed = jnp.concatenate([dqm, dkm, dv], 1)
        sig = p["sig"]
        dtotal = dmixed * (sig * (1.0 + p["total"] * (1.0 - sig)))
        draw = dtotal * taps[count - 1 : count]
        terms = [None] * count
        terms[count - 1] = colsum(dtotal * p["raw"])
        for offset in range(1, count):
            keep, shifted = p["kept"][offset - 1]
            own = jnp.where(keep, dtotal, 0.0)
            terms[count - 1 - offset] = colsum(own * shifted)
            own = own * taps[count - 1 - offset : count - offset]
            draw = draw + pltpu.roll(own, length - offset, 0)
        taps_grad = taps_grad + jnp.concatenate(terms, 0)
        tail = jnp.where(lane == 0, drate, jnp.where(lane == 1, dwrite, 0.0))
        cot = jnp.concatenate([draw, dgate, tail], 1).astype(cot_ref.dtype)
        for part in range(parts):
            cot_ref[parts * s + (part ^ odd)] = cot[part * rows_each : (part + 1) * rows_each]
    taps_grad_ref[...] = taps_grad
    lanes = lax.broadcasted_iota(jnp.int32, (1, LANES), 1)
    head = jnp.where(lanes == 0, scale_grad, jnp.where(lanes == 1, bias_grad, 0.0))
    small_ref[...] = jnp.concatenate([gain_grad, head], 1)


VMEM_SPEC = pl.BlockSpec(memory_space=pltpu.VMEM)
SMEM_SPEC = pl.BlockSpec(memory_space=pltpu.SMEM)


def mixer_forward(odd, joined, seg, taps, head, gain, sizes):
    pieces, rows_each, _ = joined.shape
    length = 2 * rows_each
    count = pieces // 2
    return pl.pallas_call(
        partial(mixer_forward_kernel, sizes),
        out_shape=(
            jax.ShapeDtypeStruct((pieces, rows_each, sizes[1]), bf16),
            jax.ShapeDtypeStruct((count, length, length), f32),
            jax.ShapeDtypeStruct((count, length, sum(sizes)), f32),
        ),
        in_specs=[SMEM_SPEC] + [VMEM_SPEC] * 5,
        out_specs=(VMEM_SPEC,) * 3,
        cost_estimate=pl.CostEstimate(flops=400_000_000, bytes_accessed=3_000_000, transcendentals=0),
        name="mixer_forward",
    )(odd, joined, seg, taps, head, gain)


def mixer_backward(odd, joined, seg, taps, head, gain, inverse, solved, dy, sizes):
    pieces, rows_each, width = joined.shape
    return pl.pallas_call(
        partial(mixer_backward_kernel, sizes),
        out_shape=(
            jax.ShapeDtypeStruct((pieces, rows_each, width), bf16),
            jax.ShapeDtypeStruct(taps.shape, f32),
            jax.ShapeDtypeStruct((1, sizes[1] + LANES), f32),
        ),
        in_specs=[SMEM_SPEC] + [VMEM_SPEC] * 8,
        out_specs=(VMEM_SPEC,) * 3,
        cost_estimate=pl.CostEstimate(flops=800_000_000, bytes_accessed=4_000_000, transcendentals=0),
        name="mixer_backward",
    )(odd, joined, seg, taps, head, gain, inverse, solved, dy)


def xor_order(pieces, index):
    pieces = list(pieces)
    bit = 1
    while bit < len(pieces):
        flip = (index & bit) != 0
        pieces = [jnp.where(flip, pieces[i ^ bit], pieces[i]) for i in range(len(pieces))]
        bit = bit * 2
    return pieces


def xor_permute(value, axis, k):
    return lax.ppermute(value, axis, [(i, i ^ k) for i in range(lax.axis_size(axis))])


def swap(value):
    return lax.ppermute(value, "section", [(0, 1), (1, 0)])


def routes():
    cores, chips = lax.axis_size("section"), lax.axis_size("dp")
    per = chips // cores
    tables = []
    for k in range(chips):
        table = []
        for s in range(cores):
            for d in range(chips):
                j = (d % per) * cores + s
                table.append((s * chips + d, (d // per) * chips + (j ^ k)))
        tables.append(table)
    return tables


def spread_out(own):
    return jnp.stack([lax.ppermute(own, ("section", "dp"), table) for table in routes()])


def collected(pieces):
    total = 0.0
    for k, table in enumerate(routes()):
        back = [(target, source) for source, target in table]
        total = total + lax.ppermute(pieces[k], ("section", "dp"), back).astype(f32)
    return total


def dot(left, right):
    return jnp.dot(left, right, preferred_element_type=f32)


def dot_t(left, right):
    return lax.dot_general(left, right, (((1,), (1,)), ((), ())), preferred_element_type=f32)


def tdot(left, right):
    return lax.dot_general(left, right, (((0,), (0,)), ((), ())), preferred_element_type=f32)


def norm_forward(value, gain):
    scale = lax.rsqrt(jnp.mean(value * value, -1, keepdims=True) + 1e-06)
    unit = value * scale
    return (unit * gain).astype(bf16), unit, scale


def norm_backward(cot, unit, scale, gain):
    gained = cot * gain
    return scale * (gained - unit * jnp.mean(gained * unit, -1, keepdims=True)), jnp.sum(cot * unit, 0)


def shards(
    tokens, segments, cotangent, norm_gains, proj_weight, rate_weight, out_weight, up_weight,
    down_weight, conv_kernels, head_params, out_gain,
):
    cores, planes, chips = (lax.axis_size(a) for a in ("section", "fsdp", "dp"))
    s, f, d = (lax.axis_index(a) for a in ("section", "fsdp", "dp"))
    first = s == 0
    seq, width = tokens.shape[2], tokens.shape[3]
    rows_own = seq // cores
    heads = head_params.shape[2] // chips
    value_dim = out_gain.shape[1] * heads
    channels = conv_kernels.shape[2] // chips
    key_dim = (channels - value_dim) // 2
    sizes = (key_dim, value_dim)
    ff = down_weight.shape[2] // chips
    keys_all, values_all = key_dim * chips, value_dim * chips
    block = width // planes
    part = block // cores

    def mine(array, start, size):
        return lax.dynamic_slice_in_dim(array, start + d * size, size, array.ndim - 1)

    proj_columns = (
        (0, key_dim), (keys_all, key_dim), (2 * keys_all, value_dim), (2 * keys_all + values_all, value_dim)
    )
    w = proj_weight[0]
    spare = LANES - 4
    rate_all = rate_weight[0]
    first_block = jnp.concatenate(
        [mine(w, start, size) for start, size in proj_columns]
        + [mine(rate_all, 0, heads), mine(rate_all, heads * chips, heads), norm_gains[0].T]
        + [jnp.zeros((block, spare), bf16), mine(out_weight[0], 0, value_dim)],
        1,
    )
    second_block = jnp.concatenate(
        [mine(up_weight[0], 0, ff), mine(up_weight[0], ff * chips, ff), mine(down_weight[0], 0, ff)], 1
    )
    joined_width = 2 * key_dim + 2 * value_dim + LANES
    gain_at = joined_width - LANES + 2

    def halves(array):
        kept = lax.dynamic_slice_in_dim(array, s * part, part, 0)
        given = lax.dynamic_slice_in_dim(array, (1 - s) * part, part, 0)
        taken = swap(given)
        return jnp.where(first, kept, taken), jnp.where(first, taken, kept)

    def gathered(half):
        own = jnp.concatenate([half] + [xor_permute(half, "fsdp", k) for k in range(1, planes)], 0)
        other = swap(own)
        return jnp.concatenate([jnp.where(first, own, other), jnp.where(first, other, own)], 0)

    first_halves, second_halves = halves(first_block), halves(second_block)
    weights = [(gathered(first_halves[i]), gathered(second_halves[i])) for i in range(2)]

    def both(array):
        other = swap(array)
        return jnp.where(first, array, other), jnp.where(first, other, array)

    taps_own = jnp.concatenate(
        [
            mine(conv_kernels[0], 0, key_dim),
            mine(conv_kernels[0], keys_all, key_dim),
            mine(conv_kernels[0], 2 * keys_all, value_dim),
        ],
        1,
    )
    taps = both(taps_own)
    heads_both = both(mine(head_params[0], 0, 1))
    gains_both = both(out_gain[0][None])

    def to_held(value):
        split = value.reshape(value.shape[0], planes, cores, part)
        ordered = jnp.stack(xor_order([split[:, i] for i in range(planes)], f), 1)
        return jnp.swapaxes(ordered, 1, 2).reshape(value.shape)

    def from_held(value):
        split = jnp.swapaxes(value.reshape(value.shape[0], cores, planes, part), 1, 2)
        ordered = jnp.stack(xor_order([split[:, i] for i in range(planes)], f), 1)
        return ordered.reshape(value.shape)

    def own_rows(array):
        return lax.dynamic_slice_in_dim(array, s * rows_own, rows_own, 0)

    stream_in = to_held(own_rows(tokens[0, 0]).astype(f32))
    dy = to_held(own_rows(cotangent[0, 0]))
    odd = (d % cores).astype(jnp.int32)[None]
    seg = spread_out(own_rows(segments[0, 0][:, None]))
    pieces = chips

    def flat(value):
        return value.reshape(-1, value.shape[-1])

    def cut(value):
        return value.reshape(pieces, rows_own, value.shape[-1])

    outputs, saved = [], []
    entering = stream_in
    for i in range(2):
        first_w, second_w = weights[i]
        joined_w, out_w = first_w[:, :joined_width], first_w[:, joined_width:]
        up_w, down_w = second_w[:, : 2 * ff], second_w[:, 2 * ff :]
        gain_one = first_w[:, gain_at].astype(f32)
        gain_two = first_w[:, gain_at + 1].astype(f32)
        hidden, unit_one, scale_one = norm_forward(entering, gain_one)
        hidden_one = flat(spread_out(hidden))
        joined = cut(dot(hidden_one, joined_w))
        mixed, inverse, solved = mixer_forward(
            odd, joined, seg, taps[i], heads_both[i], gains_both[i], sizes
        )
        mixed_half = flat(mixed)
        stream = entering + collected(cut(dot_t(mixed_half, out_w).astype(bf16)))
        hidden, unit_two, scale_two = norm_forward(stream, gain_two)
        hidden_two = flat(spread_out(hidden))
        gate_up = dot(hidden_two, up_w)
        gate, up = gate_up[:, :ff], gate_up[:, ff:]
        sig = jax.nn.sigmoid(gate)
        act_half = (gate * sig * up).astype(bf16)
        leaving = (stream + collected(cut(dot_t(act_half, down_w).astype(bf16)))).astype(bf16)
        outputs.append(leaving)
        entering = leaving.astype(f32)
        saved.append(
            (unit_one, scale_one, hidden_one, joined, inverse, solved, mixed_half, unit_two, scale_two,
             hidden_two, gate, up, act_half, gain_one, gain_two)
        )

    def half_of(value, which):
        size = width // cores
        return lax.dynamic_slice_in_dim(value, which * size, size, 1)

    def reduced(pairs, extra=None):
        def product(which):
            made = jnp.concatenate([tdot(half_of(a, which), b) for a, b in pairs], 1)
            if extra is not None:
                column, at = extra
                place = lax.broadcasted_iota(jnp.int32, made.shape, 1)
                for n in range(column.shape[0]):
                    own = lax.dynamic_slice_in_dim(column[n], which * (width // cores), width // cores, 0)
                    made = jnp.where(place == at + n, own[:, None], made)
            return made

        taken = swap(product(1 - s).astype(bf16))
        total = (product(s) + taken.astype(f32)).astype(bf16).reshape(planes, part, -1)
        result = total[0].astype(f32)
        for k in range(1, planes):
            result = result + xor_permute(total[k], "fsdp", k).astype(f32)
        return result.astype(bf16)

    def shared(term):
        return jnp.stack([term] + [xor_permute(term, "dp", k) for k in range(1, chips)])

    grads_in, grads, smalls = [None, None], [None, None], [None, None]
    for i in (1, 0):
        first_w, second_w = weights[i]
        joined_w, out_w = first_w[:, :joined_width], first_w[:, joined_width:]
        up_w, down_w = second_w[:, : 2 * ff], second_w[:, 2 * ff :]
        (unit_one, scale_one, hidden_one, joined, inverse, solved, mixed_half, unit_two, scale_two,
         hidden_two, gate, up, act_half, gain_one, gain_two) = saved[i]
        dout_half = flat(spread_out(dy.astype(bf16)))
        dact = dot(dout_half, down_w)
        sig = jax.nn.sigmoid(gate)
        dgate = dact * up * (sig * (1.0 + gate * (1.0 - sig)))
        gate_up_cot = jnp.concatenate([dgate, dact * gate * sig], 1).astype(bf16)
        cot = collected(cut(dot_t(gate_up_cot, up_w).astype(bf16)))
        back, gain_two_grad = norm_backward(cot, unit_two, scale_two, gain_two)
        stream_grad = dy + back
        branch_cot = flat(spread_out(stream_grad.astype(bf16)))
        dmixed = cut(dot(branch_cot, out_w))
        joined_cot, taps_grad, small = mixer_backward(
            odd, joined, seg, taps[i], heads_both[i], gains_both[i], inverse, solved, dmixed, sizes
        )
        joined_cot = flat(joined_cot)
        cot = collected(cut(dot_t(joined_cot, joined_w).astype(bf16)))
        back, gain_one_grad = norm_backward(cot, unit_one, scale_one, gain_one)
        dy = stream_grad + back
        grads_in[i] = dy
        second_grad = shared(reduced([(hidden_two, gate_up_cot), (dout_half, act_half)]))
        first_grad = shared(
            reduced(
                [(hidden_one, joined_cot), (branch_cot, mixed_half)],
                (jnp.stack([gain_one_grad, gain_two_grad]), gain_at),
            )
        )
        grads[i] = (first_grad, second_grad)
        smalls[i] = jnp.concatenate([taps_grad.reshape(-1), small.reshape(-1)]).reshape(-1, LANES)

    def own_layer(pair):
        kept = jnp.where(first, pair[0], pair[1])
        taken = swap(jnp.where(first, pair[1], pair[0]))
        return jnp.where(first, kept, taken), jnp.where(first, taken, kept)

    section_output = jnp.concatenate(own_layer([from_held(o) for o in outputs]), 0)
    input_grad = jnp.concatenate(own_layer([from_held(g) for g in grads_in]), 0)

    def columns_of(n):
        top, bottom = own_layer([grads[0][n], grads[1][n]])
        whole = jnp.concatenate([top, bottom], 1)
        return xor_order([whole[k] for k in range(chips)], d)

    first_grad, second_grad = columns_of(0), columns_of(1)

    def laid(members, start, size):
        return jnp.concatenate([m[:, start : start + size] for m in members], 1).astype(f32)

    place, proj_parts = 0, []
    for _, size in proj_columns:
        proj_parts.append(laid(first_grad, place, size))
        place = place + size
    proj_grad = jnp.concatenate(proj_parts, 1)
    rate_grad = jnp.concatenate([laid(first_grad, place, heads), laid(first_grad, place + heads, heads)], 1)
    gains_grad = sum(m[:, gain_at : gain_at + 2].astype(f32) for m in first_grad).T
    out_grad = laid(first_grad, joined_width, value_dim)
    up_grad = jnp.concatenate([laid(second_grad, 0, ff), laid(second_grad, ff, ff)], 1)
    down_grad = laid(second_grad, 2 * ff, ff)

    top, bottom = own_layer(smalls)
    own = top + bottom
    over_planes = xor_order([own] + [xor_permute(own, "fsdp", k) for k in range(1, planes)], f)
    own = sum(over_planes[1:], over_planes[0])
    members = xor_order([own] + [xor_permute(own, "dp", k) for k in range(1, chips)], d)
    members = [m.reshape(-1) for m in members]
    tap_count = conv_kernels.shape[1]
    tap_grads = [m[: tap_count * channels].reshape(tap_count, channels) for m in members]
    kernel_grad = jnp.concatenate(
        [m[:, :key_dim] for m in tap_grads]
        + [m[:, key_dim : 2 * key_dim] for m in tap_grads]
        + [m[:, 2 * key_dim :] for m in tap_grads],
        1,
    )
    rest = [m[tap_count * channels :] for m in members]
    out_gain_grad = sum((m[:value_dim] for m in rest[1:]), rest[0][:value_dim])
    head_grad = jnp.stack([m[value_dim : value_dim + 2] for m in rest], 1)

    return (
        section_output[None, None, None],
        input_grad[None, None, None],
        gains_grad[None],
        proj_grad[None],
        rate_grad[None],
        out_grad[None],
        up_grad[None],
        down_grad[None],
        kernel_grad[None],
        head_grad[None],
        out_gain_grad[None],
    )


def solution(mesh):
    return jax.shard_map(
        shards,
        mesh=mesh,
        in_specs=(
            P(None, ("fsdp", "dp"), None, None),
            P(None, ("fsdp", "dp"), None),
            P(None, ("fsdp", "dp"), None, None),
            P("section", None, "fsdp"),
            P("section", "fsdp", None),
            P("section", "fsdp", None),
            P("section", "fsdp", None),
            P("section", "fsdp", None),
            P("section", "fsdp", None),
            P("section", None, None),
            P("section", None, None),
            P("section", None),
        ),
        out_specs=(
            P("section", None, ("fsdp", "dp"), None, None),
            P("section", None, ("fsdp", "dp"), None, None),
            P("section", None, "fsdp"),
            P("section", "fsdp", None),
            P("section", "fsdp", None),
            P("section", "fsdp", None),
            P("section", "fsdp", None),
            P("section", "fsdp", None),
            P("section", None, None),
            P("section", None, None),
            P("section", None),
        ),
        check_vma=False,
    )
```

```python
from functools import partial

import jax
import jax.numpy as jnp
from jax import lax
from jax.experimental import pallas as pl
from jax.experimental.pallas import tpu as pltpu
from jax.sharding import PartitionSpec as P


SPAN = 64
LANES = 128

reset_level = -30.0
bf16 = jnp.bfloat16
f32 = jnp.float32


def dots(left, right, dims):
    return lax.dot_general(
        left, right, (dims, ((), ())), precision=lax.Precision.HIGHEST, preferred_element_type=f32
    )


def mm(left, right):
    return dots(left, right, ((1,), (0,)))


def mt(left, right):
    return dots(left, right, ((1,), (1,)))


def tm(left, right):
    return dots(left, right, ((0,), (0,)))


def rowsum(value):
    return jnp.sum(value, -1, keepdims=True)


def colsum(value):
    return jnp.sum(value, 0, keepdims=True)


def sequence_of(ref, q, odd, parts):
    return jnp.concatenate([ref[parts * q + (p ^ odd)] for p in range(parts)], 0)


def masks_of(length):
    rows = lax.broadcasted_iota(jnp.int32, (length, length), 0)
    columns = lax.broadcasted_iota(jnp.int32, (length, length), 1)
    same = (rows // SPAN) == (columns // SPAN)
    return rows, columns, same & (rows >= columns), same & (rows > columns), rows == columns, same


def conv_of(raw, seg, taps):
    length, count = raw.shape[0], taps.shape[0]
    places = lax.broadcasted_iota(jnp.int32, (length, 1), 0)
    total = raw * taps[count - 1 : count]
    kept = []
    for offset in range(1, count):
        shifted = pltpu.roll(raw, offset, 0)
        keep = (places >= offset) & (pltpu.roll(seg, offset, 0) == seg)
        kept.append((keep, shifted))
        total = total + jnp.where(keep, shifted, 0.0) * taps[count - 1 - offset : count - offset]
    return total, kept


def softplus(value):
    return jnp.maximum(value, 0.0) + jnp.log1p(jnp.exp(-jnp.abs(value)))


def prepared(joined, seg, taps, scale_log, bias, sizes, masks):
    key_dim, value_dim = sizes
    channels = 2 * key_dim + value_dim
    _, _, lower, _, eye, same = masks
    length = joined.shape[0]
    raw = joined[:, :channels]
    gate = joined[:, channels : channels + value_dim]
    tail = joined[:, channels + value_dim :]
    total, kept = conv_of(raw, seg, taps)
    sig = jax.nn.sigmoid(total)
    mixed = total * sig
    qm, km, v = mixed[:, :key_dim], mixed[:, key_dim : 2 * key_dim], mixed[:, 2 * key_dim :]
    rq = lax.rsqrt(rowsum(qm * qm) + 1e-06)
    rk = lax.rsqrt(rowsum(km * km) + 1e-06)
    q = qm * rq * key_dim ** (-0.5)
    k = km * rk
    beta = jax.nn.sigmoid(tail[:, 1:2])
    pre = tail[:, 0:1] + bias
    places = lax.broadcasted_iota(jnp.int32, (length, 1), 0)
    start = (places == 0) | (pltpu.roll(seg, 1, 0) != seg)
    free_decay = -jnp.exp(scale_log) * softplus(pre)
    decay = jnp.where(start, reset_level, free_decay)
    decay_row = colsum(jnp.where(eye, decay, 0.0))
    lev = rowsum(jnp.where(lower, decay_row, 0.0))
    fin = rowsum(jnp.where(same, decay_row, 0.0))
    lev_row = colsum(jnp.where(eye, lev, 0.0))
    spread = jnp.exp(jnp.where(lower, lev - lev_row, -1e30))
    grow = jnp.exp(lev)
    left = jnp.exp(fin - lev)
    return dict(
        raw=raw, gate=gate, total=total, kept=kept, sig=sig, rq=rq, rk=rk, q=q, k=k, v=v, beta=beta,
        pre=pre, start=start, free_decay=free_decay, spread=spread, grow=grow, left=left, fin=fin,
        bk=k * beta,
    )


def advance(p, solved, scores, key_dim, length):
    memory, memories, updates, outs = None, [], [], []
    for block in range(length // SPAN):
        part = slice(block * SPAN, (block + 1) * SPAN)
        update = solved[part, key_dim:]
        if memory is not None:
            update = update - mm(solved[part, :key_dim], memory)
        out = mm(scores[part, part], update)
        if memory is not None:
            out = out + mm((p["q"] * p["grow"])[part], memory)
        memories.append(memory)
        updates.append(update)
        outs.append(out)
        if (block + 1) * SPAN < length:
            grown = tm((p["k"] * p["left"])[part], update)
            if memory is not None:
                grown = grown + memory * jnp.exp(p["fin"][block * SPAN : block * SPAN + 1])
            memory = grown
    return memories, updates, jnp.concatenate(outs, 0)


def mixer_forward_kernel(sizes, odd_ref, joined_ref, seg_ref, taps_ref, head_ref, gain_ref,
                         out_ref, inverse_ref, solved_ref):
    key_dim, _ = sizes
    pieces, rows_each, _ = joined_ref.shape
    parts = 2
    length = parts * rows_each
    odd = odd_ref[0]
    masks = masks_of(length)
    rows, columns, _, strict, eye, _ = masks
    taps = taps_ref[...]
    scale_log, bias = head_ref[0:1, :], head_ref[1:2, :]
    for s in range(pieces // parts):
        joined = sequence_of(joined_ref, s, odd, parts)
        seg = sequence_of(seg_ref, s, odd, parts)
        p = prepared(joined, seg, taps, scale_log, bias, sizes, masks)
        system = jnp.where(strict, mt(p["bk"], p["k"]) * p["spread"], 0.0)
        inverse = None
        half = 1
        while half < SPAN:
            joins = ((rows // half) % 2 == 1) & (columns // half == rows // half - 1)
            corner = jnp.where(joins, system, 0.0)
            if inverse is None:
                inverse = jnp.where(eye, 1.0, 0.0) - corner
            else:
                inverse = inverse - mm(inverse, mm(corner, inverse))
            half = half * 2
        solved = mm(inverse, jnp.concatenate([p["bk"] * p["grow"], p["v"] * p["beta"]], 1))
        scores = mt(p["q"], p["k"]) * p["spread"]
        _, _, o = advance(p, solved, scores, key_dim, length)
        o = o * lax.rsqrt(jnp.mean(o * o, -1, keepdims=True) + 1e-05) * gain_ref[...]
        y = (o * (p["gate"] * jax.nn.sigmoid(p["gate"]))).astype(out_ref.dtype)
        inverse_ref[s] = inverse
        solved_ref[s] = solved
        for part in range(parts):
            out_ref[parts * s + (part ^ odd)] = y[part * rows_each : (part + 1) * rows_each]


def mixer_backward_kernel(sizes, odd_ref, joined_ref, seg_ref, taps_ref, head_ref, gain_ref,
                          inverse_ref, solved_ref, dy_ref, cot_ref, taps_grad_ref, small_ref):
    key_dim, value_dim = sizes
    pieces, rows_each, width = joined_ref.shape
    parts = 2
    length = parts * rows_each
    odd = odd_ref[0]
    masks = masks_of(length)
    rows, columns, _, strict, eye, same = masks
    taps = taps_ref[...]
    count = taps.shape[0]
    scale_log, bias = head_ref[0:1, :], head_ref[1:2, :]
    taps_grad = jnp.zeros(taps.shape, f32)
    gain_grad = jnp.zeros((1, value_dim), f32)
    scale_grad = jnp.zeros((1, 1), f32)
    bias_grad = jnp.zeros((1, 1), f32)
    lane = lax.broadcasted_iota(jnp.int32, (length, width - 2 * key_dim - 2 * value_dim), 1)
    for s in range(pieces // parts):
        joined = sequence_of(joined_ref, s, odd, parts)
        seg = sequence_of(seg_ref, s, odd, parts)
        dy = sequence_of(dy_ref, s, odd, parts)
        p = prepared(joined, seg, taps, scale_log, bias, sizes, masks)
        q, k, v, bk, beta, grow, left = (p[n] for n in ("q", "k", "v", "bk", "beta", "grow", "left"))
        inverse, solved = inverse_ref[s], solved_ref[s]
        gram = mt(bk, k) * p["spread"]
        scores = mt(q, k) * p["spread"]
        memories, updates, o = advance(p, solved, scores, key_dim, length)
        r = lax.rsqrt(jnp.mean(o * o, -1, keepdims=True) + 1e-05)
        on = o * r
        gate_sig = jax.nn.sigmoid(p["gate"])
        gate_act = p["gate"] * gate_sig
        gained = dy * gain_ref[...]
        gain_grad = gain_grad + colsum(dy * on * gate_act)
        dgate = gained * on * (gate_sig * (1.0 + p["gate"] * (1.0 - gate_sig)))
        don = gained * gate_act
        do = r * (don - on * jnp.mean(don * on, -1, keepdims=True))
        fading, carried = q * grow, k * left
        dmemory = None
        zeros_k = jnp.zeros((SPAN, key_dim), f32)
        dfading, dsolved, dscores, dcarried, dfin = [], [], [], [], []
        blocks = length // SPAN
        for block in reversed(range(blocks)):
            part = slice(block * SPAN, (block + 1) * SPAN)
            memory, update, dout = memories[block], updates[block], do[part]
            dupdate = tm(scores[part, part], dout)
            dfin_own = jnp.zeros((1, 1), f32)
            dcarried_own = zeros_k
            later = dmemory
            if later is not None:
                dupdate = dupdate + mm(carried[part], later)
                dcarried_own = mt(update, later)
            dscores_own = mt(dout, update)
            fill = [jnp.zeros((SPAN, SPAN), f32)] * blocks
            fill[block] = dscores_own
            if memory is not None:
                dfading_own = mt(dout, memory)
                dkeys_own = -mt(dupdate, memory)
                dmemory = tm(fading[part], dout) - tm(solved[part, :key_dim], dupdate)
                if later is not None:
                    fade = jnp.exp(p["fin"][block * SPAN : block * SPAN + 1])
                    dmemory = dmemory + later * fade
                    dfin_own = colsum(rowsum(later * memory)) * fade
            else:
                dfading_own, dkeys_own = zeros_k, zeros_k
            dfading.insert(0, dfading_own)
            dsolved.insert(0, jnp.concatenate([dkeys_own, dupdate], 1))
            dscores.insert(0, jnp.concatenate(fill, 1))
            dcarried.insert(0, dcarried_own)
            dfin.insert(0, jnp.broadcast_to(dfin_own, (SPAN, 1)))
        dfading, dsolved, dscores, dcarried, dfin = (
            jnp.concatenate(own, 0) for own in (dfading, dsolved, dscores, dcarried, dfin)
        )
        right = tm(inverse, dsolved)
        dsystem = -jnp.where(strict, mt(right, solved), 0.0)
        right_k, right_v = right[:, :key_dim], right[:, key_dim:]
        dlev = rowsum(right_k * bk) * grow
        dbk = right_k * grow
        dv = right_v * beta
        dbeta = rowsum(right_v * v)
        dgram = dsystem * p["spread"]
        dbk = dbk + mm(dgram, k)
        dk = tm(dgram, bk)
        dinner = dscores * p["spread"]
        dq = mm(dinner, k) + dfading * grow
        dk = dk + tm(dinner, q)
        dlevel = dsystem * gram + dscores * scores
        dlev = dlev + rowsum(dlevel) - rowsum(jnp.where(eye, colsum(dlevel), 0.0))
        dlev = dlev + rowsum(dfading * fading)
        spent = rowsum(dcarried * carried)
        dk = dk + dcarried * left
        dlev = dlev - spent
        dk = dk + dbk * beta
        dbeta = dbeta + rowsum(dbk * k)
        spent_row = colsum(jnp.where(eye, spent, 0.0))
        dlev_row = colsum(jnp.where(eye, dlev, 0.0))
        upper = same & (rows <= columns)
        ddecay = rowsum(jnp.where(upper, dlev_row, 0.0)) + rowsum(jnp.where(same, spent_row, 0.0)) + dfin
        ddecay = jnp.where(p["start"], 0.0, ddecay)
        drate = ddecay * -jnp.exp(scale_log) * jax.nn.sigmoid(p["pre"])
        scale_grad = scale_grad + colsum(ddecay * p["free_decay"])
        bias_grad = bias_grad + colsum(drate)
        dwrite = dbeta * beta * (1.0 - beta)
        qn = q * key_dim**0.5
        dqm = p["rq"] * key_dim ** (-0.5) * (dq - qn * rowsum(dq * qn))
        dkm = p["rk"] * (dk - k * rowsum(dk * k))
        dmixed = jnp.concatenate([dqm, dkm, dv], 1)
        sig = p["sig"]
        dtotal = dmixed * (sig * (1.0 + p["total"] * (1.0 - sig)))
        draw = dtotal * taps[count - 1 : count]
        terms = [None] * count
        terms[count - 1] = colsum(dtotal * p["raw"])
        for offset in range(1, count):
            keep, shifted = p["kept"][offset - 1]
            own = jnp.where(keep, dtotal, 0.0)
            terms[count - 1 - offset] = colsum(own * shifted)
            own = own * taps[count - 1 - offset : count - offset]
            draw = draw + pltpu.roll(own, length - offset, 0)
        taps_grad = taps_grad + jnp.concatenate(terms, 0)
        tail = jnp.where(lane == 0, drate, jnp.where(lane == 1, dwrite, 0.0))
        cot = jnp.concatenate([draw, dgate, tail], 1).astype(cot_ref.dtype)
        for part in range(parts):
            cot_ref[parts * s + (part ^ odd)] = cot[part * rows_each : (part + 1) * rows_each]
    taps_grad_ref[...] = taps_grad
    lanes = lax.broadcasted_iota(jnp.int32, (1, LANES), 1)
    head = jnp.where(lanes == 0, scale_grad, jnp.where(lanes == 1, bias_grad, 0.0))
    small_ref[...] = jnp.concatenate([gain_grad, head], 1)


VMEM_SPEC = pl.BlockSpec(memory_space=pltpu.VMEM)
SMEM_SPEC = pl.BlockSpec(memory_space=pltpu.SMEM)


def mixer_forward(odd, joined, seg, taps, head, gain, sizes):
    pieces, rows_each, _ = joined.shape
    length = 2 * rows_each
    count = pieces // 2
    return pl.pallas_call(
        partial(mixer_forward_kernel, sizes),
        out_shape=(
            jax.ShapeDtypeStruct((pieces, rows_each, sizes[1]), bf16),
            jax.ShapeDtypeStruct((count, length, length), f32),
            jax.ShapeDtypeStruct((count, length, sum(sizes)), f32),
        ),
        in_specs=[SMEM_SPEC] + [VMEM_SPEC] * 5,
        out_specs=(VMEM_SPEC,) * 3,
        cost_estimate=pl.CostEstimate(flops=400_000_000, bytes_accessed=3_000_000, transcendentals=0),
        name="mixer_forward",
    )(odd, joined, seg, taps, head, gain)


def mixer_backward(odd, joined, seg, taps, head, gain, inverse, solved, dy, sizes):
    pieces, rows_each, width = joined.shape
    return pl.pallas_call(
        partial(mixer_backward_kernel, sizes),
        out_shape=(
            jax.ShapeDtypeStruct((pieces, rows_each, width), bf16),
            jax.ShapeDtypeStruct(taps.shape, f32),
            jax.ShapeDtypeStruct((1, sizes[1] + LANES), f32),
        ),
        in_specs=[SMEM_SPEC] + [VMEM_SPEC] * 8,
        out_specs=(VMEM_SPEC,) * 3,
        cost_estimate=pl.CostEstimate(flops=800_000_000, bytes_accessed=4_000_000, transcendentals=0),
        name="mixer_backward",
    )(odd, joined, seg, taps, head, gain, inverse, solved, dy)


def xor_order(pieces, index):
    pieces = list(pieces)
    bit = 1
    while bit < len(pieces):
        flip = (index & bit) != 0
        pieces = [jnp.where(flip, pieces[i ^ bit], pieces[i]) for i in range(len(pieces))]
        bit = bit * 2
    return pieces


def tied(*values):
    return lax.optimization_barrier(values)


def xor_permute(value, axis, k):
    return lax.ppermute(value, axis, [(i, i ^ k) for i in range(lax.axis_size(axis))])


def swap(value):
    return lax.ppermute(value, "section", [(0, 1), (1, 0)])


def flipped(value, k, size):
    result, bit = 0, 1
    while bit < size:
        digit = (value // bit) % 2
        result = result + bit * ((1 - digit) if k & bit else digit)
        bit = bit * 2
    return result


def peers_of(cores, chips):
    s, d = lax.axis_index("section"), lax.axis_index("dp")
    per = chips // cores
    group, place = d // per, (d % per) * cores + s
    found = []
    for k in range(chips):
        target = {"section": group, "dp": flipped(place, k, chips)}
        j = flipped(d, k, chips)
        source = {"section": j % cores, "dp": s * per + j // cores}
        found.append((target, source, (target["section"] == s) & (target["dp"] == d)))
    return found


MESH_ID = pl.DeviceIdType.MESH


def exchange_kernel(cores, chips, collects, spreads, inputs, body, *refs):
    refs = list(refs)
    pieces_ref = refs.pop(0) if collects else None
    in_refs, refs = refs[:inputs], refs[inputs:]
    out_spread_ref = refs.pop(0) if spreads else None
    scratch = 2 * (collects + spreads) + collects + 2 * spreads
    out_refs, scratch_refs = refs[: len(refs) - scratch], refs[len(refs) - scratch :]
    scratch_refs = list(scratch_refs)
    if collects:
        landing_ref, send_c, recv_c = scratch_refs[:3]
        scratch_refs = scratch_refs[3:]
    if spreads:
        holding_ref, spread_ref, send_s, recv_s = scratch_refs
    peers = peers_of(cores, chips)
    barrier = pltpu.get_barrier_semaphore()
    awaited = 0
    for target, source, own in peers:
        awaited = awaited + jnp.where(own, 0, int(collects) + int(spreads))

        @pl.when(jnp.logical_not(own))
        def _():
            if spreads:
                pl.semaphore_signal(barrier, inc=1, device_id=source, device_id_type=MESH_ID)
            if collects:
                pl.semaphore_signal(barrier, inc=1, device_id=target, device_id_type=MESH_ID)

    pl.semaphore_wait(barrier, awaited)

    def transfers(make):
        for k, (target, source, own) in enumerate(peers):
            copy = make(k, target, source)

            @pl.when(jnp.logical_not(own))
            def _():
                copy.start()

    def waits(make):
        for k, (target, source, own) in enumerate(peers):
            copy = make(k, target, source)

            @pl.when(jnp.logical_not(own))
            def _():
                copy.wait()

    def collect_copy(k, target, source):
        return pltpu.make_async_remote_copy(
            src_ref=pieces_ref.at[k], dst_ref=landing_ref.at[k], send_sem=send_c.at[k],
            recv_sem=recv_c.at[k], device_id=source, device_id_type=MESH_ID,
        )

    def spread_copy(k, target, source):
        return pltpu.make_async_remote_copy(
            src_ref=holding_ref, dst_ref=spread_ref.at[k], send_sem=send_s.at[k],
            recv_sem=recv_s.at[k], device_id=target, device_id_type=MESH_ID,
        )

    total = None
    if collects:
        transfers(collect_copy)
        for k, (_, _, own) in enumerate(peers):

            @pl.when(own)
            def _():
                landing_ref[k] = pieces_ref[k]

        waits(collect_copy)
        total = landing_ref[0].astype(f32)
        for k in range(1, chips):
            total = total + landing_ref[k].astype(f32)
    sent = body(total, in_refs, out_refs)
    if spreads:
        holding_ref[...] = sent
        transfers(spread_copy)
        for k, (_, _, own) in enumerate(peers):

            @pl.when(own)
            def _():
                spread_ref[k] = sent

        waits(spread_copy)
        out_spread_ref[...] = spread_ref[...]


def exchanged(body, number, pieces, inputs, outs, spreads):
    cores, chips = lax.axis_size("section"), lax.axis_size("dp")
    collects = pieces is not None
    own = inputs[0].shape
    shape = (chips,) + own
    sems = [pltpu.SemaphoreType.DMA((chips,))] * 2
    scratch = []
    if collects:
        scratch += [pltpu.VMEM(shape, bf16)] + sems
    if spreads:
        scratch += [pltpu.VMEM(own, bf16), pltpu.VMEM(shape, bf16)] + sems
    out_shape = ([jax.ShapeDtypeStruct(shape, bf16)] if spreads else []) + list(outs)
    operands = ([pieces] if collects else []) + list(inputs)
    return pl.pallas_call(
        partial(exchange_kernel, cores, chips, collects, spreads, len(inputs), body),
        out_shape=tuple(out_shape),
        in_specs=[VMEM_SPEC] * len(operands),
        out_specs=(VMEM_SPEC,) * len(out_shape),
        scratch_shapes=scratch,
        compiler_params=pltpu.CompilerParams(collective_id=number, has_side_effects=True),
        cost_estimate=pl.CostEstimate(flops=1_000_000, bytes_accessed=20_000_000, transcendentals=0),
    )(*operands)


def unit_of(value):
    scale = lax.rsqrt(jnp.mean(value * value, -1, keepdims=True) + 1e-06)
    return value * scale, scale


def enter_body(total, ins, outs):
    unit, _ = unit_of(ins[0][...])
    return (unit * ins[1][...]).astype(bf16)


def middle_body(total, ins, outs):
    stream = ins[0][...] + total
    outs[0][...] = stream
    unit, _ = unit_of(stream)
    return (unit * ins[1][...]).astype(bf16)


def relay_body(total, ins, outs):
    stream = (ins[0][...] + total).astype(bf16).astype(f32)
    outs[0][...] = stream
    unit, _ = unit_of(stream)
    return (unit * ins[1][...]).astype(bf16)


def leave_body(total, ins, outs):
    outs[0][...] = ins[0][...] + total


def turn_body(total, ins, outs):
    return ins[0][...].astype(bf16)


def back_body(total, ins, outs):
    unit, scale = unit_of(ins[1][...])
    gained = total * ins[2][...]
    grad = ins[0][...] + scale * (gained - unit * jnp.mean(gained * unit, -1, keepdims=True))
    outs[0][...] = grad
    outs[1][...] = colsum(total * unit)
    return grad.astype(bf16)


def routes():
    cores, chips = lax.axis_size("section"), lax.axis_size("dp")
    per = chips // cores
    tables = []
    for k in range(chips):
        table = []
        for s in range(cores):
            for d in range(chips):
                j = (d % per) * cores + s
                table.append((s * chips + d, (d // per) * chips + (j ^ k)))
        tables.append(table)
    return tables


def dot(left, right):
    return jnp.dot(left, right, preferred_element_type=f32)


def dot_t(left, right):
    return lax.dot_general(left, right, (((1,), (1,)), ((), ())), preferred_element_type=f32)


def tdot(left, right):
    return lax.dot_general(left, right, (((0,), (0,)), ((), ())), preferred_element_type=f32)


def shards(
    tokens, segments, cotangent, norm_gains, proj_weight, rate_weight, out_weight, up_weight,
    down_weight, conv_kernels, head_params, out_gain,
):
    cores, planes, chips = (lax.axis_size(a) for a in ("section", "fsdp", "dp"))
    s, f, d = (lax.axis_index(a) for a in ("section", "fsdp", "dp"))
    first = s == 0
    seq, width = tokens.shape[2], tokens.shape[3]
    rows_own = seq // cores
    heads = head_params.shape[2] // chips
    value_dim = out_gain.shape[1] * heads
    channels = conv_kernels.shape[2] // chips
    key_dim = (channels - value_dim) // 2
    sizes = (key_dim, value_dim)
    ff = down_weight.shape[2] // chips
    keys_all, values_all = key_dim * chips, value_dim * chips
    block = width // planes
    part = block // cores

    def mine(array, start, size):
        return lax.dynamic_slice_in_dim(array, start + d * size, size, array.ndim - 1)

    proj_columns = (
        (0, key_dim), (keys_all, key_dim), (2 * keys_all, value_dim), (2 * keys_all + values_all, value_dim)
    )
    w = proj_weight[0]
    spare = LANES - 4
    rate_all = rate_weight[0]
    first_block = jnp.concatenate(
        [mine(w, start, size) for start, size in proj_columns]
        + [mine(rate_all, 0, heads), mine(rate_all, heads * chips, heads), norm_gains[0].T]
        + [jnp.zeros((block, spare), bf16), mine(out_weight[0], 0, value_dim)],
        1,
    )
    second_block = jnp.concatenate(
        [mine(up_weight[0], 0, ff), mine(up_weight[0], ff * chips, ff), mine(down_weight[0], 0, ff)], 1
    )
    joined_width = 2 * key_dim + 2 * value_dim + LANES
    gain_at = joined_width - LANES + 2

    def halves(array):
        kept = lax.dynamic_slice_in_dim(array, s * part, part, 0)
        given = lax.dynamic_slice_in_dim(array, (1 - s) * part, part, 0)
        taken = swap(given)
        return jnp.where(first, kept, taken), jnp.where(first, taken, kept)

    def gathered(half):
        return [half] + [xor_permute(half, "fsdp", k) for k in range(1, planes)]

    def completed(members):
        own = jnp.concatenate(members, 0)
        other = swap(own)
        return jnp.concatenate([jnp.where(first, own, other), jnp.where(first, other, own)], 0)

    first_halves, second_halves = halves(first_block), halves(second_block)
    members = {}
    members["a", 0] = gathered(first_halves[0])
    second_half, *members["a", 0] = tied(second_halves[0], *members["a", 0])
    members["m", 0] = gathered(second_half)
    weights = [[completed(members["a", 0]), None], [None, None]]

    def both(array):
        other = swap(array)
        return jnp.where(first, array, other), jnp.where(first, other, array)

    taps_own = jnp.concatenate(
        [
            mine(conv_kernels[0], 0, key_dim),
            mine(conv_kernels[0], keys_all, key_dim),
            mine(conv_kernels[0], 2 * keys_all, value_dim),
        ],
        1,
    )
    taps = both(taps_own)
    heads_both = both(mine(head_params[0], 0, 1))
    gains_both = both(out_gain[0][None])

    def to_held(value):
        split = value.reshape(value.shape[0], planes, cores, part)
        ordered = jnp.stack(xor_order([split[:, i] for i in range(planes)], f), 1)
        return jnp.swapaxes(ordered, 1, 2).reshape(value.shape)

    def from_held(value):
        split = jnp.swapaxes(value.reshape(value.shape[0], cores, planes, part), 1, 2)
        ordered = jnp.stack(xor_order([split[:, i] for i in range(planes)], f), 1)
        return ordered.reshape(value.shape)

    def own_rows(array):
        return lax.dynamic_slice_in_dim(array, s * rows_own, rows_own, 0)

    stream_in = to_held(own_rows(tokens[0, 0]).astype(f32))
    dy = to_held(own_rows(cotangent[0, 0]))
    odd = (d % cores).astype(jnp.int32)[None]
    seg_own = own_rows(segments[0, 0][:, None])
    seg = jnp.stack([lax.ppermute(seg_own, ("section", "dp"), table) for table in routes()])
    pieces = chips

    def flat(value):
        return value.reshape(-1, value.shape[-1])

    def cut(value):
        return value.reshape(pieces, rows_own, value.shape[-1])

    row = jax.ShapeDtypeStruct(stream_in.shape, f32)
    line = jax.ShapeDtypeStruct((1, width), f32)

    def gain_of(i, n):
        return weights[i][0][:, gain_at + n].astype(f32)[None]

    outputs, saved = [], []
    entering = stream_in
    (spread,) = exchanged(enter_body, 1, None, (entering, gain_of(0, 0)), (), True)
    for i in range(2):
        first_w = weights[i][0]
        joined_w, out_w = first_w[:, :joined_width], first_w[:, joined_width:]
        hidden_one = flat(spread)
        joined = cut(dot(hidden_one, joined_w))
        mixed, inverse, solved = mixer_forward(
            odd, joined, seg, taps[i], heads_both[i], gains_both[i], sizes
        )
        mixed, *members["m", i] = tied(mixed, *members["m", i])
        mixed_half = flat(mixed)
        if i == 0:
            first_half, second_half, *members["m", 0] = tied(
                first_halves[1], second_halves[1], *members["m", 0]
            )
            members["a", 1] = gathered(first_half)
            second_half, *members["a", 1] = tied(second_half, *members["a", 1])
            members["m", 1] = gathered(second_half)
        weights[i][1] = completed(members["m", i])
        second_w = weights[i][1]
        up_w, down_w = second_w[:, : 2 * ff], second_w[:, 2 * ff :]
        spread, stream = exchanged(
            middle_body, 2, cut(dot_t(mixed_half, out_w).astype(bf16)), (entering, gain_of(i, 1)),
            (row,), True,
        )
        hidden_two = flat(spread)
        gate_up = dot(hidden_two, up_w)
        gate, up = gate_up[:, :ff], gate_up[:, ff:]
        sig = jax.nn.sigmoid(gate)
        act_half = (gate * sig * up).astype(bf16)
        if i == 0:
            act_half, *members["a", 1] = tied(act_half, *members["a", 1])
            weights[1][0] = completed(members["a", 1])
        saved.append((entering, stream, hidden_one, joined, inverse, solved, mixed_half, hidden_two, gate, up, act_half))
        partial_out = cut(dot_t(act_half, down_w).astype(bf16))
        if i == 0:
            spread, entering = exchanged(relay_body, 3, partial_out, (stream, gain_of(1, 0)), (row,), True)
        else:
            (entering,) = exchanged(leave_body, 4, partial_out, (stream,), (row,), False)
        outputs.append(entering.astype(bf16))

    def half_of(value, which):
        size = width // cores
        return lax.dynamic_slice_in_dim(value, which * size, size, 1)

    def reduced(pairs, extra=None):
        def product(which):
            made = jnp.concatenate([tdot(half_of(a, which), b) for a, b in pairs], 1)
            if extra is not None:
                column, at = extra
                place = lax.broadcasted_iota(jnp.int32, made.shape, 1)
                for n in range(column.shape[0]):
                    own = lax.dynamic_slice_in_dim(column[n], which * (width // cores), width // cores, 0)
                    made = jnp.where(place == at + n, own[:, None], made)
            return made

        taken = swap(product(1 - s).astype(bf16))
        total = (product(s) + taken.astype(f32)).astype(bf16).reshape(planes, part, -1)
        return [total[0]] + [xor_permute(total[k], "fsdp", k) for k in range(1, planes)]

    def summed(members):
        result = members[0].astype(f32)
        for member in members[1:]:
            result = result + member.astype(f32)
        return result.astype(bf16)

    def shared(term):
        return [term] + [xor_permute(term, "dp", k) for k in range(1, chips)]

    grads_in, grads, smalls = [None, None], [None, None], [None, None]
    (spread,) = exchanged(turn_body, 5, None, (dy,), (), True)
    for i in (1, 0):
        first_w, second_w = weights[i]
        joined_w, out_w = first_w[:, :joined_width], first_w[:, joined_width:]
        up_w, down_w = second_w[:, : 2 * ff], second_w[:, 2 * ff :]
        (entered, stream, hidden_one, joined, inverse, solved, mixed_half, hidden_two, gate, up, act_half) = saved[i]
        dout_half = flat(spread)
        dact = dot(dout_half, down_w)
        sig = jax.nn.sigmoid(gate)
        dgate = dact * up * (sig * (1.0 + gate * (1.0 - sig)))
        gate_up_cot = jnp.concatenate([dgate, dact * gate * sig], 1).astype(bf16)
        spread, stream_grad, gain_two_grad = exchanged(
            back_body, 6, cut(dot_t(gate_up_cot, up_w).astype(bf16)), (dy, stream, gain_of(i, 1)),
            (row, line), True,
        )
        branch_cot = flat(spread)
        dmixed = cut(dot(branch_cot, out_w))
        second_members = reduced([(hidden_two, gate_up_cot), (dout_half, act_half)])
        joined_cot, taps_grad, small = mixer_backward(
            odd, joined, seg, taps[i], heads_both[i], gains_both[i], inverse, solved, dmixed, sizes
        )
        joined_cot = flat(joined_cot)
        back_in = cut(dot_t(joined_cot, joined_w).astype(bf16))
        operands = (stream_grad, entered, gain_of(i, 0))
        if i == 1:
            spread, dy, gain_one_grad = exchanged(back_body, 6, back_in, operands, (row, line), True)
        else:
            dy, gain_one_grad = exchanged(back_body, 7, back_in, operands, (row, line), False)
        grads_in[i] = dy
        second_grad = shared(summed(second_members))
        first_members = reduced(
            [(hidden_one, joined_cot), (branch_cot, mixed_half)],
            (jnp.concatenate([gain_one_grad, gain_two_grad], 0), gain_at),
        )
        grads[i] = [shared(summed(first_members)), second_grad]
        smalls[i] = jnp.concatenate([taps_grad.reshape(-1), small.reshape(-1)]).reshape(-1, LANES)

    def own_layer(pair):
        kept = jnp.where(first, pair[0], pair[1])
        taken = swap(jnp.where(first, pair[1], pair[0]))
        return jnp.where(first, kept, taken), jnp.where(first, taken, kept)

    section_output = jnp.concatenate(own_layer([from_held(o) for o in outputs]), 0)
    input_grad = jnp.concatenate(own_layer([from_held(g) for g in grads_in]), 0)

    def columns_of(n):
        top, bottom = own_layer([jnp.stack(grads[0][n]), jnp.stack(grads[1][n])])
        whole = jnp.concatenate([top, bottom], 1)
        return xor_order([whole[k] for k in range(chips)], d)

    first_grad, second_grad = columns_of(0), columns_of(1)

    def laid(members, start, size):
        return jnp.concatenate([m[:, start : start + size] for m in members], 1).astype(f32)

    place, proj_parts = 0, []
    for _, size in proj_columns:
        proj_parts.append(laid(first_grad, place, size))
        place = place + size
    proj_grad = jnp.concatenate(proj_parts, 1)
    rate_grad = jnp.concatenate([laid(first_grad, place, heads), laid(first_grad, place + heads, heads)], 1)
    gains_grad = sum(m[:, gain_at : gain_at + 2].astype(f32) for m in first_grad).T
    out_grad = laid(first_grad, joined_width, value_dim)
    up_grad = jnp.concatenate([laid(second_grad, 0, ff), laid(second_grad, ff, ff)], 1)
    down_grad = laid(second_grad, 2 * ff, ff)

    top, bottom = own_layer(smalls)
    own = top + bottom
    over_planes = xor_order([own] + [xor_permute(own, "fsdp", k) for k in range(1, planes)], f)
    own = sum(over_planes[1:], over_planes[0])
    members = xor_order([own] + [xor_permute(own, "dp", k) for k in range(1, chips)], d)
    members = [m.reshape(-1) for m in members]
    tap_count = conv_kernels.shape[1]
    tap_grads = [m[: tap_count * channels].reshape(tap_count, channels) for m in members]
    kernel_grad = jnp.concatenate(
        [m[:, :key_dim] for m in tap_grads]
        + [m[:, key_dim : 2 * key_dim] for m in tap_grads]
        + [m[:, 2 * key_dim :] for m in tap_grads],
        1,
    )
    rest = [m[tap_count * channels :] for m in members]
    out_gain_grad = sum((m[:value_dim] for m in rest[1:]), rest[0][:value_dim])
    head_grad = jnp.stack([m[value_dim : value_dim + 2] for m in rest], 1)

    return (
        section_output[None, None, None],
        input_grad[None, None, None],
        gains_grad[None],
        proj_grad[None],
        rate_grad[None],
        out_grad[None],
        up_grad[None],
        down_grad[None],
        kernel_grad[None],
        head_grad[None],
        out_gain_grad[None],
    )


def solution(mesh):
    return jax.shard_map(
        shards,
        mesh=mesh,
        in_specs=(
            P(None, ("fsdp", "dp"), None, None),
            P(None, ("fsdp", "dp"), None),
            P(None, ("fsdp", "dp"), None, None),
            P("section", None, "fsdp"),
            P("section", "fsdp", None),
            P("section", "fsdp", None),
            P("section", "fsdp", None),
            P("section", "fsdp", None),
            P("section", "fsdp", None),
            P("section", None, None),
            P("section", None, None),
            P("section", None),
        ),
        out_specs=(
            P("section", None, ("fsdp", "dp"), None, None),
            P("section", None, ("fsdp", "dp"), None, None),
            P("section", None, "fsdp"),
            P("section", "fsdp", None),
            P("section", "fsdp", None),
            P("section", "fsdp", None),
            P("section", "fsdp", None),
            P("section", "fsdp", None),
            P("section", None, None),
            P("section", None, None),
            P("section", None),
        ),
        check_vma=False,
    )
```
